768 devices in a mesh: elem: 96 (over z_lo, y, core), band: 8 (over z_hi, x).
Axes of the slice: x: 4, y: 8, z: 12 (z_hi: 2, z_lo: 6; z = z_hi * 6 + z_lo), core: 2. Of those that a mesh axis runs over, the one named last changes fastest.
Arguments:
- orbitals: bfloat16 [96, 512, 13824], P('elem', 'band'), may hold values from -6 to 6
- potential: float32 [96, 13824], P('elem'), may hold values from 0 to 1.9
- basis_count: int32 [96], P('elem'), may hold values from 256 to 512, as said below
- states: bfloat16 [96, 512, 1024], P('elem', None, 'band'), may hold values from -6 to 6
Outputs:
- filtered_states: bfloat16 [96, 512, 1024], P('elem', None, 'band')
The draws below stay inside these ranges and needn't reach their ends.
Inputs may be any that keep to these rules, and one draw needn't show every extreme that they name: `basis_count`: some element keeps all 512 basis functions and some element keeps 512 // 2 of them in every draw.
All inputs are finite; a program needn't handle non-finite values.
Results may differ from the reference program's by a relative error of at most 0.03.
Values may be sent and summed in bfloat16 or wider, within the bound.
No kernel may reach another device: no remote copies, remote signals or barrier semaphores. Data moves between devices by JAX's collectives and lax.ppermute only.
A program may use at most 32 MiB of HBM per device.

```python
from functools import partial
import jax
import jax.numpy as jnp
from jax import lax

NB = 512
P_SIZE = 24
G = 13824
DEG = 2
EB = 4
NS = 1024
ELEMS = 96
N_BAND = 8


def draw_basis_count(key, part):
    first_key, second_key = jax.random.split(key)
    counts = jax.random.randint(first_key, (ELEMS,), NB // 2, NB + 1, dtype=jnp.int32)
    shuffled = jax.random.permutation(second_key, ELEMS)
    counts = counts.at[shuffled[0]].set(NB)
    counts = counts.at[shuffled[1]].set(NB // 2)
    return counts


def level_of(stream_key, dims, cuts, low, high):
    def one(axis_at, parts):
        steps = jax.random.uniform(jax.random.fold_in(jax.random.fold_in(stream_key, 6), axis_at), (parts,), jnp.float32, low / len(cuts), high / len(cuts))
        return jnp.repeat(jnp.exp(steps), dims[axis_at] // parts).reshape((-1,) + (1,) * (len(dims) - axis_at - 1))

    level = one(*cuts[0])
    for cut in cuts[1:]:
        level = level * one(*cut)
    return level


def centred(stream_key, dims, width, reach, shards=(), kind=jnp.bfloat16):
    result = width * jax.random.normal(stream_key, dims, jnp.float32)
    if shards:
        result = result * level_of(stream_key, dims, shards, -0.22, 0.18)
    return jnp.clip(result, -reach, reach).astype(kind)


def setup_inputs(seed: int = 0) -> dict:
    key_list = jax.random.split(jax.random.key(seed), 5)
    orbitals = centred(key_list[0], (ELEMS, NB, G), 1.0, 6.0, ((0, 96), (1, 8)))
    potential = jnp.clip(1.9 * jax.random.uniform(key_list[1], (ELEMS, G), jnp.float32) ** level_of(key_list[1], (ELEMS, G), ((0, 96),), -0.2, 0.2), 0.0, 1.9)
    basis_count = draw_basis_count(jax.random.fold_in(key_list[4], 71), 0)
    states = centred(key_list[3], (ELEMS, NB, NS), 1.0, 6.0, ((0, 96), (2, 8)))
    return dict(orbitals=orbitals, potential=potential, basis_count=basis_count, states=states)


LOW_EDGE = 4.0
HIGH_EDGE = 14.0
PENALTY = 1.0
SHIFT_CENTER = 4.0
HALF_WIDTH = 6.0
HIGHEST = lax.Precision.HIGHEST

def laplace_apply(values):
    padded = jnp.pad(values, ((0, 0), (1, 1), (1, 1), (1, 1)))
    beside = padded[:, 2:, 1:-1, 1:-1] + padded[:, :-2, 1:-1, 1:-1]
    beside = beside + padded[:, 1:-1, 2:, 1:-1] + padded[:, 1:-1, :-2, 1:-1]
    beside = beside + padded[:, 1:-1, 1:-1, 2:] + padded[:, 1:-1, 1:-1, :-2]
    return 6.0 * values - beside

def hamiltonian(values, potential):
    return laplace_apply(values) + potential * values

def filtered(orbitals, potential, kept_count, start_index):
    orbital_count = orbitals.shape[0]
    layout = (orbital_count, P_SIZE, P_SIZE, P_SIZE)
    cube_potential = potential.reshape(P_SIZE, P_SIZE, P_SIZE)
    middle = 0.5 * (HIGH_EDGE + LOW_EDGE)
    spread = 0.5 * (HIGH_EDGE - LOW_EDGE)
    previous = orbitals.astype(jnp.float32).reshape(layout)
    current = (hamiltonian(previous, cube_potential) - middle * previous) / spread
    for repeat in range(DEG - 1):
        following = 2.0 * (hamiltonian(current, cube_potential) - middle * current) / spread - previous
        previous, current = (current, following)
    magnitude = jnp.sqrt(lax.optimization_barrier(jnp.mean(current * current, axis=(1, 2, 3), keepdims=True)) + 1e-06)
    active = start_index + jnp.arange(orbital_count, dtype=jnp.int32) < kept_count
    basis = jnp.where(active[:, None, None, None], current / magnitude, 0.0).astype(jnp.bfloat16)
    applied = hamiltonian(basis.astype(jnp.float32), cube_potential).astype(jnp.bfloat16)
    return (basis.reshape(orbital_count, -1), applied.reshape(orbital_count, -1))

def face_pair(gridded, axis_place, upper):
    extent = gridded.shape[axis_place]
    surface = lax.index_in_dim(gridded, extent - 1 if upper else 0, axis_place, keepdims=False)
    beneath = lax.index_in_dim(gridded, extent - 2 if upper else 1, axis_place, keepdims=False)
    return (surface, beneath)

def face_terms(own_surface, own_beneath, other_surface, other_beneath):
    own_slope = own_surface - own_beneath
    other_slope = other_surface - other_beneath
    leading = jnp.concatenate([-PENALTY * own_surface + 0.5 * own_slope, 0.5 * own_surface], axis=-1)
    trailing = jnp.concatenate([other_surface, other_slope], axis=-1)
    return (leading, trailing)

def filter_one(packed):
    orbitals, potential, kept_count = packed
    return filtered(orbitals, potential, kept_count, 0)

def element_blocks(basis_all, applied_all, element):
    directions = [(1, 1, True, False), (-1, 1, False, True), (EB, 0, True, False), (-EB, 0, False, True)]
    planes = P_SIZE // N_BAND
    own = basis_all[element].astype(jnp.float32).reshape(NB, N_BAND, planes, P_SIZE, P_SIZE)
    own_applied = applied_all[element].astype(jnp.float32).reshape(NB, N_BAND, -1)
    interior = jnp.einsum('asg,bsg->sab', own.reshape(NB, N_BAND, -1), own_applied, precision=HIGHEST) * (1.0 / G)
    partials = [interior]
    for offset, axis_code, own_upper, other_upper in directions:
        neighbour = (element + offset) % ELEMS
        other = basis_all[neighbour].astype(jnp.float32).reshape(NB, N_BAND, planes, P_SIZE, P_SIZE)
        own_surface, own_beneath = face_pair(own, 3 + axis_code, own_upper)
        other_surface, other_beneath = face_pair(other, 3 + axis_code, other_upper)
        leading, trailing = face_terms(own_surface.reshape(NB, N_BAND, -1), own_beneath.reshape(NB, N_BAND, -1), other_surface.reshape(NB, N_BAND, -1), other_beneath.reshape(NB, N_BAND, -1))
        partials.append(jnp.einsum('asf,bsf->sab', leading, trailing, precision=HIGHEST) * (1.0 / (P_SIZE * P_SIZE)))
    stacked = jnp.stack(partials)
    rounded = lax.optimization_barrier(stacked.astype(jnp.bfloat16)).astype(jnp.float32)
    return lax.optimization_barrier(jnp.sum(rounded, axis=1)).astype(jnp.bfloat16)

def apply_all(blocks, current):
    offsets = [0, 1, -1, EB, -EB]

    def one_element(element):
        running = jnp.zeros((NB, current.shape[2]), jnp.float32)
        for position, offset in enumerate(offsets):
            source = current[(element + offset) % ELEMS]
            running = running + jnp.dot(blocks[element, position].astype(jnp.float32), source.astype(jnp.float32), preferred_element_type=jnp.float32)
        return running
    return lax.map(one_element, jnp.arange(ELEMS, dtype=jnp.int32))

def scaled(blocks, current):
    return (apply_all(blocks, current) - SHIFT_CENTER * current.astype(jnp.float32)) / HALF_WIDTH

def reference(orbitals, potential, basis_count, states):
    basis_all, applied_all = lax.map(filter_one, (orbitals, potential, basis_count))
    blocks = lax.map(partial(element_blocks, basis_all, applied_all), jnp.arange(ELEMS, dtype=jnp.int32))
    first_term = scaled(blocks, states).astype(jnp.bfloat16)
    second_term = (2.0 * scaled(blocks, first_term) - states.astype(jnp.float32)).astype(jnp.bfloat16)
    third_term = 2.0 * scaled(blocks, second_term) - first_term.astype(jnp.float32)
    magnitude = jnp.sqrt(lax.optimization_barrier(jnp.mean(third_term * third_term, axis=1, keepdims=True)) + 1e-06)
    return (third_term / magnitude).astype(jnp.bfloat16)
```

```python
import jax
import jax.numpy as jnp
import numpy as np
from jax import lax
from jax.sharding import Mesh, PartitionSpec as P

P_SIZE = 24
PLANE = P_SIZE * P_SIZE
G = 13824
EB = 4
HALVES = 2
SLABS = 4
CHUNKS = 4

LOW_EDGE = 4.0
HIGH_EDGE = 14.0
SHIFT_CENTER = 4.0
HALF_WIDTH = 6.0
MIDDLE = 0.5 * (HIGH_EDGE + LOW_EDGE)
SPREAD = 0.5 * (HIGH_EDGE - LOW_EDGE)


def from_behind(value, axis, by):
    devices = lax.axis_size(axis)
    return lax.ppermute(value, axis, [(i, (i + by) % devices) for i in range(devices)])


def swap_halves(value):
    return lax.ppermute(value, "half", [(0, 1), (1, 0)])


def side_masks(length):
    where = jnp.arange(length, dtype=jnp.int32)
    zpos = where % P_SIZE
    ypos = where // P_SIZE % P_SIZE
    return (
        (zpos < P_SIZE - 1).astype(jnp.float32),
        (zpos > 0).astype(jnp.float32),
        (ypos < P_SIZE - 1).astype(jnp.float32),
        (ypos > 0).astype(jnp.float32),
    )


def flat_hamiltonian(padded, length, potential, masks):
    values = padded[:, PLANE : PLANE + length]
    beside = padded[:, 2 * PLANE : 2 * PLANE + length] + padded[:, 0:length]
    beside = beside + masks[0] * padded[:, PLANE + 1 : PLANE + 1 + length]
    beside = beside + masks[1] * padded[:, PLANE - 1 : PLANE - 1 + length]
    beside = beside + masks[2] * padded[:, PLANE + P_SIZE : PLANE + P_SIZE + length]
    beside = beside + masks[3] * padded[:, PLANE - P_SIZE : PLANE - P_SIZE + length]
    return 6.0 * values - beside + potential * values


def whole_hamiltonian(values, potential, masks):
    padded = jnp.pad(values, ((0, 0), (PLANE, PLANE)))
    return flat_hamiltonian(padded, values.shape[1], potential, masks)


def filtered_basis(orbitals, potential, kept_count, start_index):
    orbital_count = orbitals.shape[0]
    masks = side_masks(G)
    previous = orbitals.astype(jnp.float32)
    current = (whole_hamiltonian(previous, potential, masks) - MIDDLE * previous) / SPREAD
    current = (
        2.0 * (whole_hamiltonian(current, potential, masks) - MIDDLE * current) / SPREAD - previous
    )
    magnitude = jnp.sqrt(jnp.mean(current * current, axis=1, keepdims=True) + 1e-06)
    active = start_index + jnp.arange(orbital_count, dtype=jnp.int32) < kept_count
    return jnp.where(active[:, None], current / magnitude, 0.0).astype(jnp.bfloat16)


def face_selector(planes):
    grid = np.arange(planes * PLANE, dtype=np.int32).reshape(planes, P_SIZE, P_SIZE)
    last = P_SIZE - 1
    groups = [
        grid[:, :, 0], grid[:, :, 1], grid[:, 0, :], grid[:, 1, :],
        grid[:, :, last - 1], grid[:, :, last], grid[:, last - 1, :], grid[:, last, :],
    ]
    chosen = jnp.asarray(np.concatenate([g.reshape(-1) for g in groups]))
    points = jnp.arange(planes * PLANE, dtype=jnp.int32)
    return (chosen[:, None] == points[None, :]).astype(jnp.bfloat16)


def slab_rows(orbitals, potential, kept_count, half, band):
    per_device = orbitals.shape[0]
    step = per_device // CHUNKS
    half_points = G // HALVES
    slab_points = half_points // SLABS
    taken = half_points + PLANE
    arrived = []
    for chunk in range(CHUNKS):
        basis = filtered_basis(
            orbitals[chunk * step : (chunk + 1) * step],
            potential,
            kept_count,
            band * per_device + chunk * step,
        )
        padded = jnp.pad(basis, ((0, 0), (0, PLANE)))
        lower, upper = padded[:, :taken], padded[:, half_points:]
        kept = jnp.where(half == 0, lower, upper)
        other = swap_halves(jnp.where(half == 0, upper, lower))
        ordered = jnp.stack(
            [jnp.where(half == 0, kept, other), jnp.where(half == 0, other, kept)]
        )
        pieces = jnp.stack(
            [
                ordered[:, :, s * slab_points : (s + 1) * slab_points + PLANE]
                for s in range(SLABS)
            ]
        )
        arrived.append(lax.all_to_all(pieces, "slab", 0, 0, tiled=True))
    rows = jnp.stack(arrived, axis=2)
    return jnp.swapaxes(rows, 0, 1).reshape(-1, slab_points + PLANE)


def transposed_dot(a, b, contract_a, contract_b):
    return lax.dot_general(
        a, b, (((contract_a,), (contract_b,)), ((), ())), preferred_element_type=jnp.float32
    )


def apply_blocks(h_self, h_z, h_y, current):
    ahead_z = from_behind(current, "elem", -1)
    ahead_y = from_behind(current, "elem", -EB)
    back_z = transposed_dot(h_z, current, 0, 0).astype(jnp.bfloat16)
    back_y = transposed_dot(h_y, current, 0, 0).astype(jnp.bfloat16)
    behind_z = from_behind(back_z, "elem", 1)
    behind_y = from_behind(back_y, "elem", EB)
    running = transposed_dot(h_self, current, 1, 0)
    running = running + transposed_dot(h_z, ahead_z, 1, 0)
    running = running + transposed_dot(h_y, ahead_y, 1, 0)
    return running + behind_z.astype(jnp.float32) + behind_y.astype(jnp.float32)


def scaled(blocks, current):
    return (apply_blocks(*blocks, current) - SHIFT_CENTER * current.astype(jnp.float32)) / HALF_WIDTH


def on_device(orbitals, potential, basis_count, states):
    half = lax.axis_index("half")
    slab = lax.axis_index("slab")
    band = half * SLABS + slab
    extended = slab_rows(orbitals[0], potential[0], basis_count[0], half, band)
    total = extended.shape[0]
    length = extended.shape[1] - PLANE
    planes = length // PLANE
    own = extended[:, :length]

    faces = transposed_dot(face_selector(planes), own, 1, 1).astype(jnp.bfloat16)
    width = 2 * planes * P_SIZE
    other_z = from_behind(faces[:width], "elem", -1)
    other_y = from_behind(faces[width : 2 * width], "elem", -EB)

    slab_potential = lax.dynamic_slice_in_dim(potential[0], band * length, length, 0)
    padded = jnp.pad(extended.astype(jnp.float32), ((0, 0), (PLANE, 0)))
    applied = flat_hamiltonian(padded, length, slab_potential, side_masks(length))
    applied = jnp.concatenate(
        [applied.astype(jnp.bfloat16), -own[:, length - PLANE :]], axis=1
    )
    h_self = transposed_dot(extended, applied, 1, 1) * (1.0 / G)
    weight = -0.5 / PLANE
    h_z = transposed_dot(faces[2 * width : 3 * width], other_z, 0, 0) * weight
    h_y = transposed_dot(faces[3 * width :], other_y, 0, 0) * weight

    partial = jnp.stack([h_self, h_z, h_y], axis=0).astype(jnp.bfloat16)
    partial = partial.reshape(3, SLABS, total // SLABS, total).swapaxes(0, 1)
    pieces = lax.all_to_all(partial, "slab", 0, 0, tiled=True)
    summed = jnp.sum(pieces.astype(jnp.float32), axis=0).astype(jnp.bfloat16)
    swapped = swap_halves(summed)
    summed = (summed.astype(jnp.float32) + swapped.astype(jnp.float32)).astype(jnp.bfloat16)
    blocks = lax.all_gather(summed, "slab", axis=1, tiled=True)
    blocks = (blocks[0], blocks[1], blocks[2])

    start = states[0]
    first = scaled(blocks, start).astype(jnp.bfloat16)
    second = (2.0 * scaled(blocks, first) - start.astype(jnp.float32)).astype(jnp.bfloat16)
    third = 2.0 * scaled(blocks, second) - first.astype(jnp.float32)
    magnitude = jnp.sqrt(jnp.mean(third * third, axis=0, keepdims=True) + 1e-06)
    return (third / magnitude).astype(jnp.bfloat16)[None]


def solution(mesh):
    elems, bands = mesh.devices.shape
    inner = Mesh(mesh.devices.reshape(elems, HALVES, bands // HALVES), ("elem", "half", "slab"))
    both = ("half", "slab")
    placed = (P("elem", both, None), P("elem", None), P("elem"), P("elem", None, both))
    return jax.shard_map(
        on_device, mesh=inner, in_specs=placed, out_specs=P("elem", None, both), check_vma=False
    )
```

```python
import jax
import jax.numpy as jnp
import numpy as np
from jax import lax
from jax.sharding import Mesh, PartitionSpec as P

P_SIZE = 24
PLANE = P_SIZE * P_SIZE
G = 13824
EB = 4
HALVES = 2
SLABS = 4
CHUNKS = 4

LOW_EDGE = 4.0
HIGH_EDGE = 14.0
SHIFT_CENTER = 4.0
HALF_WIDTH = 6.0
MIDDLE = 0.5 * (HIGH_EDGE + LOW_EDGE)
SPREAD = 0.5 * (HIGH_EDGE - LOW_EDGE)


def from_behind(value, axis, by):
    devices = lax.axis_size(axis)
    return lax.ppermute(value, axis, [(i, (i + by) % devices) for i in range(devices)])


def swap_halves(value):
    return lax.ppermute(value, "half", [(0, 1), (1, 0)])


def side_masks(length):
    where = jnp.arange(length, dtype=jnp.int32)
    zpos = where % P_SIZE
    ypos = where // P_SIZE % P_SIZE
    return (
        (zpos < P_SIZE - 1).astype(jnp.float32),
        (zpos > 0).astype(jnp.float32),
        (ypos < P_SIZE - 1).astype(jnp.float32),
        (ypos > 0).astype(jnp.float32),
    )


def flat_hamiltonian(padded, length, potential, masks):
    values = padded[:, PLANE : PLANE + length]
    beside = padded[:, 2 * PLANE : 2 * PLANE + length] + padded[:, 0:length]
    beside = beside + masks[0] * padded[:, PLANE + 1 : PLANE + 1 + length]
    beside = beside + masks[1] * padded[:, PLANE - 1 : PLANE - 1 + length]
    beside = beside + masks[2] * padded[:, PLANE + P_SIZE : PLANE + P_SIZE + length]
    beside = beside + masks[3] * padded[:, PLANE - P_SIZE : PLANE - P_SIZE + length]
    return 6.0 * values - beside + potential * values


def whole_hamiltonian(values, potential, masks):
    padded = jnp.pad(values, ((0, 0), (PLANE, PLANE)))
    return flat_hamiltonian(padded, values.shape[1], potential, masks)


def filtered_basis(orbitals, potential, kept_count, start_index):
    orbital_count = orbitals.shape[0]
    masks = side_masks(G)
    previous = orbitals.astype(jnp.float32)
    current = (whole_hamiltonian(previous, potential, masks) - MIDDLE * previous) / SPREAD
    current = (
        2.0 * (whole_hamiltonian(current, potential, masks) - MIDDLE * current) / SPREAD - previous
    )
    magnitude = jnp.sqrt(jnp.mean(current * current, axis=1, keepdims=True) + 1e-06)
    active = start_index + jnp.arange(orbital_count, dtype=jnp.int32) < kept_count
    return jnp.where(active[:, None], current / magnitude, 0.0).astype(jnp.bfloat16)


def face_selector(planes):
    grid = np.arange(planes * PLANE, dtype=np.int32).reshape(planes, P_SIZE, P_SIZE)
    last = P_SIZE - 1
    groups = [
        grid[:, :, 0], grid[:, :, 1], grid[:, 0, :], grid[:, 1, :],
        grid[:, :, last - 1], grid[:, :, last], grid[:, last - 1, :], grid[:, last, :],
    ]
    chosen = jnp.asarray(np.concatenate([g.reshape(-1) for g in groups]))
    points = jnp.arange(planes * PLANE, dtype=jnp.int32)
    return (chosen[:, None] == points[None, :]).astype(jnp.bfloat16)


def transposed_dot(a, b, contract_a, contract_b):
    return lax.dot_general(
        a, b, (((contract_a,), (contract_b,)), ((), ())), preferred_element_type=jnp.float32
    )


def slab_applied(rows, length, slab_potential):
    padded = jnp.pad(rows.astype(jnp.float32), ((0, 0), (PLANE, 0)))
    applied = flat_hamiltonian(padded, length, slab_potential, side_masks(length))
    return jnp.concatenate(
        [applied.astype(jnp.bfloat16), -rows[:, length - PLANE : length]], axis=1
    )


def slab_rows(orbitals, potential, kept_count, slab_potential, half, band):
    per_device = orbitals.shape[0]
    step = per_device // CHUNKS
    half_points = G // HALVES
    slab_points = half_points // SLABS
    taken = half_points + PLANE
    arrived, applied = [], []
    tied = None
    for chunk in range(CHUNKS):
        source = orbitals[chunk * step : (chunk + 1) * step]
        if tied is not None:
            source, tied = lax.optimization_barrier((source, tied))
        basis = filtered_basis(
            source, potential, kept_count, band * per_device + chunk * step
        )
        padded = jnp.pad(basis, ((0, 0), (0, PLANE)))
        lower, upper = padded[:, :taken], padded[:, half_points:]
        kept = jnp.where(half == 0, lower, upper)
        leaving = tied = jnp.where(half == 0, upper, lower)
        other = swap_halves(leaving)
        ordered = jnp.stack(
            [jnp.where(half == 0, kept, other), jnp.where(half == 0, other, kept)]
        )
        pieces = jnp.stack(
            [
                ordered[:, :, s * slab_points : (s + 1) * slab_points + PLANE]
                for s in range(SLABS)
            ]
        )
        rows = lax.all_to_all(pieces, "slab", 0, 0, tiled=True)
        rows = lax.optimization_barrier(rows.reshape(-1, slab_points + PLANE))
        applied.append(lax.optimization_barrier(slab_applied(rows, slab_points, slab_potential)))
        arrived.append(rows)
    return jnp.concatenate(arrived), jnp.concatenate(applied)


def arrival_order(rows):
    columns = rows.shape[1]
    split = rows.reshape(HALVES, SLABS, CHUNKS, -1, columns)
    return split.transpose(2, 1, 0, 3, 4).reshape(-1, columns)


def natural_order(rows):
    columns = rows.shape[1]
    split = rows.reshape(CHUNKS, SLABS, HALVES, -1, columns)
    return split.transpose(2, 1, 0, 3, 4).reshape(-1, columns)


def pair_swap(value, by, odd):
    devices = lax.axis_size("elem")
    low = [i for i in range(devices) if (i // by) % 2 == odd]
    pairs = [(i, (i + by) % devices) for i in low]
    return lax.ppermute(value, "elem", pairs + [(j, i) for i, j in pairs])


def exchange(value, product, by):
    even = (lax.axis_index("elem") // by) % 2 == 0
    from_odd = pair_swap(jnp.where(even, value, product), by, 1)
    from_even = pair_swap(jnp.where(even, product, value), by, 0)
    ahead = jnp.where(even, from_even, from_odd)
    behind = jnp.where(even, from_odd, from_even)
    return ahead, behind


def neighbours_of(current, back_z, back_y):
    ahead_y, behind_y = exchange(current, back_y, EB)
    ahead_z, behind_z = exchange(current, back_z, 1)
    return ahead_z, ahead_y, behind_z, behind_y


def scaled(blocks, current, ahead=None):
    h_self, h_z, h_y = blocks
    back_y = transposed_dot(h_y, current, 0, 0).astype(jnp.bfloat16)
    back_z = transposed_dot(h_z, current, 0, 0).astype(jnp.bfloat16)
    if ahead is None:
        ahead_z, ahead_y, behind_z, behind_y = neighbours_of(current, back_z, back_y)
    else:
        ahead_z, ahead_y = ahead
        behind_y = from_behind(back_y, "elem", EB)
        behind_z = from_behind(back_z, "elem", 1)
    running = transposed_dot(h_self, current, 1, 0)
    running = running + transposed_dot(h_z, ahead_z, 1, 0)
    running = running + transposed_dot(h_y, ahead_y, 1, 0)
    running = running + behind_z.astype(jnp.float32) + behind_y.astype(jnp.float32)
    return (running - SHIFT_CENTER * current.astype(jnp.float32)) / HALF_WIDTH


def device_body(orbitals, potential, basis_count, states):
    half = lax.axis_index("half")
    slab = lax.axis_index("slab")
    band = half * SLABS + slab
    length = G // (HALVES * SLABS)
    planes = length // PLANE
    slab_potential = lax.dynamic_slice_in_dim(potential[0], band * length, length, 0)

    start = arrival_order(states[0])
    ahead = (from_behind(start, "elem", -1), from_behind(start, "elem", -EB))

    extended, applied = slab_rows(
        orbitals[0], potential[0], basis_count[0], slab_potential, half, band
    )
    total = extended.shape[0]

    faces = transposed_dot(face_selector(planes), extended[:, :length], 1, 1)
    faces = faces.astype(jnp.bfloat16)
    width = 2 * planes * P_SIZE
    other_y = from_behind(faces[width : 2 * width], "elem", -EB)
    other_z = from_behind(faces[:width], "elem", -1)
    h_self = transposed_dot(extended, applied, 1, 1) * (1.0 / G)
    weight = -0.5 / PLANE
    h_z = transposed_dot(faces[2 * width : 3 * width], other_z, 0, 0) * weight
    h_y = transposed_dot(faces[3 * width :], other_y, 0, 0) * weight

    partial = jnp.stack([h_self, h_z, h_y], axis=0).astype(jnp.bfloat16)
    partial = partial.reshape(3, SLABS, total // SLABS, total).swapaxes(0, 1)
    pieces = lax.all_to_all(partial, "slab", 0, 0, tiled=True)
    summed = jnp.sum(pieces.astype(jnp.float32), axis=0).astype(jnp.bfloat16)
    swapped = swap_halves(summed)
    summed = (summed.astype(jnp.float32) + swapped.astype(jnp.float32)).astype(jnp.bfloat16)
    copies = jnp.broadcast_to(summed[None], (SLABS,) + summed.shape)
    blocks = lax.all_to_all(copies, "slab", 0, 0, tiled=True)
    blocks = blocks.swapaxes(0, 1).reshape(3, total, total)
    blocks = (blocks[0], blocks[1], blocks[2])

    first = scaled(blocks, start, ahead).astype(jnp.bfloat16)
    second = (2.0 * scaled(blocks, first) - start.astype(jnp.float32)).astype(jnp.bfloat16)
    third = 2.0 * scaled(blocks, second) - first.astype(jnp.float32)
    magnitude = jnp.sqrt(jnp.mean(third * third, axis=0, keepdims=True) + 1e-06)
    return natural_order((third / magnitude).astype(jnp.bfloat16))[None]


def solution(mesh):
    elems, bands = mesh.devices.shape
    inner = Mesh(mesh.devices.reshape(elems, HALVES, bands // HALVES), ("elem", "half", "slab"))
    both = ("half", "slab")
    placed = (P("elem", both, None), P("elem", None), P("elem"), P("elem", None, both))
    return jax.shard_map(
        device_body, mesh=inner, in_specs=placed, out_specs=P("elem", None, both), check_vma=False
    )
```

```python
import jax
import jax.numpy as jnp
import numpy as np
from jax import lax
from jax.sharding import Mesh, PartitionSpec as P

P_SIZE = 24
PLANE = P_SIZE * P_SIZE
G = 13824
EB = 4
HALVES = 2
SLABS = 4
CHUNKS = 4
BOTH = ("half", "slab")

LOW_EDGE = 4.0
HIGH_EDGE = 14.0
SHIFT_CENTER = 4.0
HALF_WIDTH = 6.0
MIDDLE = 0.5 * (HIGH_EDGE + LOW_EDGE)
SPREAD = 0.5 * (HIGH_EDGE - LOW_EDGE)


def from_behind(value, axis, by):
    devices = lax.axis_size(axis)
    return lax.ppermute(value, axis, [(i, (i + by) % devices) for i in range(devices)])


def swap_halves(value):
    return lax.ppermute(value, "half", [(0, 1), (1, 0)])


def side_masks(length):
    where = jnp.arange(length, dtype=jnp.int32)
    zpos = where % P_SIZE
    ypos = where // P_SIZE % P_SIZE
    return (
        (zpos < P_SIZE - 1).astype(jnp.float32),
        (zpos > 0).astype(jnp.float32),
        (ypos < P_SIZE - 1).astype(jnp.float32),
        (ypos > 0).astype(jnp.float32),
    )


def flat_hamiltonian(padded, length, potential, masks):
    values = padded[:, PLANE : PLANE + length]
    beside = padded[:, 2 * PLANE : 2 * PLANE + length] + padded[:, 0:length]
    beside = beside + masks[0] * padded[:, PLANE + 1 : PLANE + 1 + length]
    beside = beside + masks[1] * padded[:, PLANE - 1 : PLANE - 1 + length]
    beside = beside + masks[2] * padded[:, PLANE + P_SIZE : PLANE + P_SIZE + length]
    beside = beside + masks[3] * padded[:, PLANE - P_SIZE : PLANE - P_SIZE + length]
    return 6.0 * values - beside + potential * values


def whole_hamiltonian(values, potential, masks):
    padded = jnp.pad(values, ((0, 0), (PLANE, PLANE)))
    return flat_hamiltonian(padded, values.shape[1], potential, masks)


def filtered_basis(orbitals, potential, kept_count, start_index):
    orbital_count = orbitals.shape[0]
    masks = side_masks(G)
    previous = orbitals.astype(jnp.float32)
    current = (whole_hamiltonian(previous, potential, masks) - MIDDLE * previous) / SPREAD
    current = (
        2.0 * (whole_hamiltonian(current, potential, masks) - MIDDLE * current) / SPREAD - previous
    )
    magnitude = jnp.sqrt(jnp.mean(current * current, axis=1, keepdims=True) + 1e-06)
    active = start_index + jnp.arange(orbital_count, dtype=jnp.int32) < kept_count
    return jnp.where(active[:, None], current / magnitude, 0.0).astype(jnp.bfloat16)


def face_selector(planes):
    grid = np.arange(planes * PLANE, dtype=np.int32).reshape(planes, P_SIZE, P_SIZE)
    last = P_SIZE - 1
    groups = [
        grid[:, :, 0], grid[:, :, 1], grid[:, 0, :], grid[:, 1, :],
        grid[:, :, last - 1], grid[:, :, last], grid[:, last - 1, :], grid[:, last, :],
    ]
    chosen = jnp.asarray(np.concatenate([g.reshape(-1) for g in groups]))
    points = jnp.arange(planes * PLANE, dtype=jnp.int32)
    return (chosen[:, None] == points[None, :]).astype(jnp.bfloat16)


def transposed_dot(a, b, contract_a, contract_b):
    return lax.dot_general(
        a, b, (((contract_a,), (contract_b,)), ((), ())), preferred_element_type=jnp.float32
    )


def owned_basis(orbitals, potential, kept_count, start_index):
    step = orbitals.shape[0] // CHUNKS
    chunks = []
    tied = None
    for chunk in range(CHUNKS):
        source = orbitals[chunk * step : (chunk + 1) * step]
        if tied is not None:
            source, tied = lax.optimization_barrier((source, tied))
            chunks[-1] = tied
        tied = filtered_basis(source, potential, kept_count, start_index + chunk * step)
        chunks.append(tied)
    return chunks


def slab_rows(chunks, length):
    slabs = [
        jnp.concatenate([c[:, s * length : (s + 1) * length] for c in chunks])
        for s in range(HALVES * SLABS)
    ]
    rows = lax.all_to_all(jnp.stack(slabs), BOTH, 0, 0, tiled=True)
    return rows.reshape(-1, length)


def pair_swap(value, by, odd):
    devices = lax.axis_size("elem")
    low = [i for i in range(devices) if (i // by) % 2 == odd]
    pairs = [(i, (i + by) % devices) for i in low]
    return lax.ppermute(value, "elem", pairs + [(j, i) for i, j in pairs])


def exchange(value, product, by):
    even = (lax.axis_index("elem") // by) % 2 == 0
    from_odd = pair_swap(jnp.where(even, value, product), by, 1)
    from_even = pair_swap(jnp.where(even, product, value), by, 0)
    ahead = jnp.where(even, from_even, from_odd)
    behind = jnp.where(even, from_odd, from_even)
    return ahead, behind


def scaled(blocks, current, given=None):
    h_self, h_z, h_y = blocks
    back_z = transposed_dot(h_z, current, 0, 0).astype(jnp.bfloat16)
    back_y = transposed_dot(h_y, current, 0, 0).astype(jnp.bfloat16)
    if given is None:
        ahead_z, behind_z = exchange(current, back_z, 1)
        ahead_y, behind_y = exchange(current, back_y, EB)
        running = transposed_dot(h_self, current, 1, 0)
    else:
        ahead_z, ahead_y, running = given
        behind_z = from_behind(back_z, "elem", 1)
        behind_y = from_behind(back_y, "elem", EB)
    running = running + transposed_dot(h_z, ahead_z, 1, 0)
    running = running + transposed_dot(h_y, ahead_y, 1, 0)
    running = running + behind_z.astype(jnp.float32) + behind_y.astype(jnp.float32)
    return (running - SHIFT_CENTER * current.astype(jnp.float32)) / HALF_WIDTH


def slices_of(partial):
    count, total, columns = partial.shape
    return partial.reshape(count, SLABS, total // SLABS, columns).swapaxes(0, 1)


def sum_over_slabs(partial):
    pieces = lax.all_to_all(slices_of(partial), "slab", 0, 0, tiled=True)
    return jnp.sum(pieces.astype(jnp.float32), axis=0).astype(jnp.bfloat16)


def sum_over_halves(summed):
    swapped = swap_halves(summed)
    return (summed.astype(jnp.float32) + swapped.astype(jnp.float32)).astype(jnp.bfloat16)


def gather_slices(summed):
    count, rows, columns = summed.shape
    copies = jnp.broadcast_to(summed[None], (SLABS,) + summed.shape)
    blocks = lax.all_to_all(copies, "slab", 0, 0, tiled=True)
    return [blocks[:, i].reshape(SLABS * rows, columns) for i in range(count)]


def device_body(orbitals, potential, basis_count, states):
    half = lax.axis_index("half")
    slab = lax.axis_index("slab")
    band = half * SLABS + slab
    length = G // (HALVES * SLABS)
    planes = length // PLANE
    slab_potential = lax.dynamic_slice_in_dim(potential[0], band * length, length, 0)

    start = states[0]
    ahead_z = from_behind(start, "elem", -1)
    ahead_y = from_behind(start, "elem", -EB)
    ahead = lax.optimization_barrier(jnp.concatenate([ahead_z, ahead_y]))
    ahead_z, ahead_y = ahead[: ahead.shape[0] // 2], ahead[ahead.shape[0] // 2 :]

    chunks = owned_basis(
        orbitals[0], potential[0], basis_count[0], band * orbitals.shape[1]
    )
    rows = slab_rows(chunks, length)

    above = lax.ppermute(
        rows[:, :PLANE], BOTH, [(i + 1, i) for i in range(HALVES * SLABS - 1)]
    )
    faces = transposed_dot(face_selector(planes), rows, 1, 1).astype(jnp.bfloat16)
    width = 2 * planes * P_SIZE
    other_z = from_behind(faces[:width], "elem", -1)
    other_y = from_behind(faces[width : 2 * width], "elem", -EB)

    padded = jnp.pad(rows.astype(jnp.float32), ((0, 0), (PLANE, PLANE)))
    applied = flat_hamiltonian(padded, length, slab_potential, side_masks(length))
    last = rows[:, length - PLANE :]
    h_self = transposed_dot(rows, applied.astype(jnp.bfloat16), 1, 1)
    h_self = h_self - transposed_dot(last, above, 1, 1) - transposed_dot(above, last, 1, 1)
    weight = -0.5 / PLANE
    h_z = transposed_dot(faces[2 * width : 3 * width], other_z, 0, 0) * weight
    h_y = transposed_dot(faces[3 * width :], other_y, 0, 0) * weight

    summed_self = sum_over_slabs((h_self * (1.0 / G)).astype(jnp.bfloat16)[None])
    whole_self = sum_over_halves(summed_self)
    summed_faces = sum_over_slabs(jnp.stack([h_z, h_y]).astype(jnp.bfloat16))
    whole_faces = sum_over_halves(summed_faces)
    (block_self,) = gather_slices(whole_self)
    running = transposed_dot(block_self, start, 1, 0)
    block_z, block_y = gather_slices(whole_faces)
    blocks = (block_self, block_z, block_y)

    first = scaled(blocks, start, (ahead_z, ahead_y, running)).astype(jnp.bfloat16)
    second = (2.0 * scaled(blocks, first) - start.astype(jnp.float32)).astype(jnp.bfloat16)
    third = 2.0 * scaled(blocks, second) - first.astype(jnp.float32)
    magnitude = jnp.sqrt(jnp.mean(third * third, axis=0, keepdims=True) + 1e-06)
    return (third / magnitude).astype(jnp.bfloat16)[None]


def solution(mesh):
    elems, bands = mesh.devices.shape
    inner = Mesh(mesh.devices.reshape(elems, HALVES, bands // HALVES), ("elem", "half", "slab"))
    placed = (P("elem", BOTH, None), P("elem", None), P("elem"), P("elem", None, BOTH))
    return jax.shard_map(
        device_body, mesh=inner, in_specs=placed, out_specs=P("elem", None, BOTH), check_vma=False
    )
```

```python
import functools

import jax
import jax.numpy as jnp
import numpy as np
from jax import lax
from jax.experimental import pallas as pl
from jax.experimental.pallas import tpu as pltpu
from jax.sharding import Mesh, PartitionSpec as P

P_SIZE = 24
PLANE = P_SIZE * P_SIZE
G = 13824
EB = 4
HALVES = 2
SLABS = 4
CHUNKS = 4
BOTH = ("half", "slab")

LOW_EDGE = 4.0
HIGH_EDGE = 14.0
SHIFT_CENTER = 4.0
HALF_WIDTH = 6.0
MIDDLE = 0.5 * (HIGH_EDGE + LOW_EDGE)
SPREAD = 0.5 * (HIGH_EDGE - LOW_EDGE)


def from_behind(value, axis, by):
    devices = lax.axis_size(axis)
    return lax.ppermute(value, axis, [(i, (i + by) % devices) for i in range(devices)])


def swap_halves(value):
    return lax.ppermute(value, "half", [(0, 1), (1, 0)])


def side_masks(length):
    where = jnp.arange(length, dtype=jnp.int32)
    zpos = where % P_SIZE
    ypos = where // P_SIZE % P_SIZE
    return (
        (zpos < P_SIZE - 1).astype(jnp.float32),
        (zpos > 0).astype(jnp.float32),
        (ypos < P_SIZE - 1).astype(jnp.float32),
        (ypos > 0).astype(jnp.float32),
    )


def flat_hamiltonian(padded, length, potential, masks):
    values = padded[:, PLANE : PLANE + length]
    beside = padded[:, 2 * PLANE : 2 * PLANE + length] + padded[:, 0:length]
    beside = beside + masks[0] * padded[:, PLANE + 1 : PLANE + 1 + length]
    beside = beside + masks[1] * padded[:, PLANE - 1 : PLANE - 1 + length]
    beside = beside + masks[2] * padded[:, PLANE + P_SIZE : PLANE + P_SIZE + length]
    beside = beside + masks[3] * padded[:, PLANE - P_SIZE : PLANE - P_SIZE + length]
    return 6.0 * values - beside + potential * values


def whole_hamiltonian(values, potential, masks):
    padded = jnp.pad(values, ((0, 0), (PLANE, PLANE)))
    return flat_hamiltonian(padded, values.shape[1], potential, masks)


def filtered_basis(orbitals, potential, kept_count, start_index):
    orbital_count = orbitals.shape[0]
    masks = side_masks(G)
    previous = orbitals.astype(jnp.float32)
    current = (whole_hamiltonian(previous, potential, masks) - MIDDLE * previous) / SPREAD
    current = (
        2.0 * (whole_hamiltonian(current, potential, masks) - MIDDLE * current) / SPREAD - previous
    )
    magnitude = jnp.sqrt(jnp.mean(current * current, axis=1, keepdims=True) + 1e-06)
    active = start_index + jnp.arange(orbital_count, dtype=jnp.int32) < kept_count
    return jnp.where(active[:, None], current / magnitude, 0.0).astype(jnp.bfloat16)


def face_selector(planes, width):
    grid = np.arange(planes * PLANE, dtype=np.int32).reshape(planes, P_SIZE, P_SIZE)
    last = P_SIZE - 1
    groups = [
        grid[:, :, 0], grid[:, :, 1], grid[:, 0, :], grid[:, 1, :],
        grid[:, :, last - 1], grid[:, :, last], grid[:, last - 1, :], grid[:, last, :],
    ]
    chosen = jnp.asarray(np.concatenate([g.reshape(-1) for g in groups]))
    points = jnp.arange(width, dtype=jnp.int32)
    return (chosen[:, None] == points[None, :]).astype(jnp.bfloat16)


def transposed_dot(a, b, contract_a, contract_b):
    return lax.dot_general(
        a, b, (((contract_a,), (contract_b,)), ((), ())), preferred_element_type=jnp.float32
    )


def owned_basis(orbitals, potential, kept_count, start_index):
    step = orbitals.shape[0] // CHUNKS
    chunks = []
    tied = None
    for chunk in range(CHUNKS):
        source = orbitals[chunk * step : (chunk + 1) * step]
        if tied is not None:
            source, tied = lax.optimization_barrier((source, tied))
            chunks[-1] = tied
        tied = filtered_basis(source, potential, kept_count, start_index + chunk * step)
        chunks.append(tied)
    return chunks


def cut_kernel(length, *refs):
    out = refs[-1]
    count, _, width = out.shape
    piece = (width - length) // 2
    middle = refs[0].shape[1] // 2
    step = refs[0].shape[0]
    for k, source in enumerate(refs[:-1]):
        rows = pl.ds(k * step, step)
        for s in range(count):
            out[s, rows, :length] = source[:, s * length : (s + 1) * length]
            low = middle - PLANE + s * piece
            out[s, rows, length : length + piece] = source[:, low : low + piece]
            out[s, rows, length + piece :] = source[:, low + PLANE : low + PLANE + piece]


def slab_rows(chunks, length):
    count = HALVES * SLABS
    width = length + 2 * (PLANE // count)
    functions = sum(c.shape[0] for c in chunks)
    whole = pl.BlockSpec(memory_space=pltpu.VMEM)
    slabs = pl.pallas_call(
        functools.partial(cut_kernel, length),
        out_shape=jax.ShapeDtypeStruct((count, functions, width), jnp.bfloat16),
        in_specs=[whole] * len(chunks),
        out_specs=whole,
        compiler_params=pltpu.CompilerParams(vmem_limit_bytes=16 << 20),
    )(*chunks)
    rows = lax.all_to_all(slabs, BOTH, 0, 0, tiled=True)
    return rows.reshape(-1, width)


def pair_swap(value, by, odd):
    devices = lax.axis_size("elem")
    low = [i for i in range(devices) if (i // by) % 2 == odd]
    pairs = [(i, (i + by) % devices) for i in low]
    return lax.ppermute(value, "elem", pairs + [(j, i) for i, j in pairs])


def exchange(value, product, by):
    even = (lax.axis_index("elem") // by) % 2 == 0
    from_odd = pair_swap(jnp.where(even, value, product), by, 1)
    from_even = pair_swap(jnp.where(even, product, value), by, 0)
    ahead = jnp.where(even, from_even, from_odd)
    behind = jnp.where(even, from_odd, from_even)
    return ahead, behind


def scaled(blocks, current, given=None):
    h_self, h_z, h_y = blocks
    back_z = transposed_dot(h_z, current, 0, 0).astype(jnp.bfloat16)
    back_y = transposed_dot(h_y, current, 0, 0).astype(jnp.bfloat16)
    if given is None:
        ahead_z, behind_z = exchange(current, back_z, 1)
        ahead_y, behind_y = exchange(current, back_y, EB)
        running = transposed_dot(h_self, current, 1, 0)
    else:
        ahead_z, ahead_y, running = given
        behind_z = from_behind(back_z, "elem", 1)
        behind_y = from_behind(back_y, "elem", EB)
    running = running + transposed_dot(h_z, ahead_z, 1, 0)
    running = running + transposed_dot(h_y, ahead_y, 1, 0)
    running = running + behind_z.astype(jnp.float32) + behind_y.astype(jnp.float32)
    return (running - SHIFT_CENTER * current.astype(jnp.float32)) / HALF_WIDTH


def slices_of(partial):
    count, total, columns = partial.shape
    return partial.reshape(count, SLABS, total // SLABS, columns).swapaxes(0, 1)


def sum_over_slabs(partial):
    pieces = lax.all_to_all(slices_of(partial), "slab", 0, 0, tiled=True)
    return jnp.sum(pieces.astype(jnp.float32), axis=0).astype(jnp.bfloat16)


def sum_over_halves(summed):
    swapped = swap_halves(summed)
    return (summed.astype(jnp.float32) + swapped.astype(jnp.float32)).astype(jnp.bfloat16)


def gather_slices(summed):
    count, rows, columns = summed.shape
    copies = jnp.broadcast_to(summed[None], (SLABS,) + summed.shape)
    blocks = lax.all_to_all(copies, "slab", 0, 0, tiled=True)
    return [blocks[:, i].reshape(SLABS * rows, columns) for i in range(count)]


def device_body(orbitals, potential, basis_count, states):
    half = lax.axis_index("half")
    slab = lax.axis_index("slab")
    band = half * SLABS + slab
    length = G // (HALVES * SLABS)
    planes = length // PLANE
    slab_potential = lax.dynamic_slice_in_dim(potential[0], band * length, length, 0)

    start = states[0]
    ahead_z = from_behind(start, "elem", -1)
    ahead_y = from_behind(start, "elem", -EB)
    ahead = lax.optimization_barrier(jnp.concatenate([ahead_z, ahead_y]))
    ahead_z, ahead_y = ahead[: ahead.shape[0] // 2], ahead[ahead.shape[0] // 2 :]

    chunks = owned_basis(
        orbitals[0], potential[0], basis_count[0], band * orbitals.shape[1]
    )
    rows = slab_rows(chunks, length)

    above = lax.ppermute(
        rows[:, :PLANE], "slab", [(i + 1, i) for i in range(SLABS - 1)]
    )
    faces = transposed_dot(face_selector(planes, rows.shape[1]), rows, 1, 1)
    faces = faces.astype(jnp.bfloat16)
    width = 2 * planes * P_SIZE
    other_z = from_behind(faces[:width], "elem", -1)
    other_y = from_behind(faces[width : 2 * width], "elem", -EB)

    padded = jnp.pad(rows[:, :length].astype(jnp.float32), ((0, 0), (PLANE, PLANE)))
    applied = flat_hamiltonian(padded, length, slab_potential, side_masks(length))
    last = rows[:, length - PLANE : length]
    piece = (rows.shape[1] - length) // 2
    below_part, above_part = rows[:, length : length + piece], rows[:, length + piece :]
    applied = jnp.concatenate(
        [applied.astype(jnp.bfloat16), -above_part, -below_part], axis=1
    )
    h_self = transposed_dot(rows, applied, 1, 1)
    h_self = h_self - transposed_dot(last, above, 1, 1) - transposed_dot(above, last, 1, 1)
    weight = -0.5 / PLANE
    h_z = transposed_dot(faces[2 * width : 3 * width], other_z, 0, 0) * weight
    h_y = transposed_dot(faces[3 * width :], other_y, 0, 0) * weight

    summed_self = sum_over_slabs((h_self * (1.0 / G)).astype(jnp.bfloat16)[None])
    whole_self = sum_over_halves(summed_self)
    summed_faces = sum_over_slabs(jnp.stack([h_z, h_y]).astype(jnp.bfloat16))
    whole_faces = sum_over_halves(summed_faces)
    (block_self,) = gather_slices(whole_self)
    running = transposed_dot(block_self, start, 1, 0)
    block_z, block_y = gather_slices(whole_faces)
    blocks = (block_self, block_z, block_y)

    first = scaled(blocks, start, (ahead_z, ahead_y, running)).astype(jnp.bfloat16)
    second = (2.0 * scaled(blocks, first) - start.astype(jnp.float32)).astype(jnp.bfloat16)
    third = 2.0 * scaled(blocks, second) - first.astype(jnp.float32)
    magnitude = jnp.sqrt(jnp.mean(third * third, axis=0, keepdims=True) + 1e-06)
    return (third / magnitude).astype(jnp.bfloat16)[None]


def solution(mesh):
    elems, bands = mesh.devices.shape
    inner = Mesh(mesh.devices.reshape(elems, HALVES, bands // HALVES), ("elem", "half", "slab"))
    placed = (P("elem", BOTH, None), P("elem", None), P("elem"), P("elem", None, BOTH))
    return jax.shard_map(
        device_body, mesh=inner, in_specs=placed, out_specs=P("elem", None, BOTH), check_vma=False
    )
```

```python
import functools

import jax
import jax.numpy as jnp
import numpy as np
from jax import lax
from jax.experimental import pallas as pl
from jax.experimental.pallas import tpu as pltpu
from jax.sharding import Mesh, PartitionSpec as P

P_SIZE = 24
PLANE = P_SIZE * P_SIZE
G = 13824
EB = 4
HALVES = 2
SLABS = 4
CHUNKS = 4
BOTH = ("half", "slab")

LOW_EDGE = 4.0
HIGH_EDGE = 14.0
SHIFT_CENTER = 4.0
HALF_WIDTH = 6.0
MIDDLE = 0.5 * (HIGH_EDGE + LOW_EDGE)
SPREAD = 0.5 * (HIGH_EDGE - LOW_EDGE)


def from_behind(value, axis, by):
    devices = lax.axis_size(axis)
    return lax.ppermute(value, axis, [(i, (i + by) % devices) for i in range(devices)])


def swap_halves(value):
    return lax.ppermute(value, "half", [(0, 1), (1, 0)])


def side_masks(length):
    where = jnp.arange(length, dtype=jnp.int32)
    zpos = where % P_SIZE
    ypos = where // P_SIZE % P_SIZE
    return (
        (zpos < P_SIZE - 1).astype(jnp.float32),
        (zpos > 0).astype(jnp.float32),
        (ypos < P_SIZE - 1).astype(jnp.float32),
        (ypos > 0).astype(jnp.float32),
    )


def flat_hamiltonian(padded, length, potential, masks):
    values = padded[:, PLANE : PLANE + length]
    beside = padded[:, 2 * PLANE : 2 * PLANE + length] + padded[:, 0:length]
    beside = beside + masks[0] * padded[:, PLANE + 1 : PLANE + 1 + length]
    beside = beside + masks[1] * padded[:, PLANE - 1 : PLANE - 1 + length]
    beside = beside + masks[2] * padded[:, PLANE + P_SIZE : PLANE + P_SIZE + length]
    beside = beside + masks[3] * padded[:, PLANE - P_SIZE : PLANE - P_SIZE + length]
    return 6.0 * values - beside + potential * values


def whole_hamiltonian(values, potential, masks):
    padded = jnp.pad(values, ((0, 0), (PLANE, PLANE)))
    return flat_hamiltonian(padded, values.shape[1], potential, masks)


def filtered_basis(orbitals, potential, kept_count, start_index):
    orbital_count = orbitals.shape[0]
    masks = side_masks(G)
    previous = orbitals.astype(jnp.float32)
    current = (whole_hamiltonian(previous, potential, masks) - MIDDLE * previous) / SPREAD
    current = (
        2.0 * (whole_hamiltonian(current, potential, masks) - MIDDLE * current) / SPREAD - previous
    )
    magnitude = jnp.sqrt(jnp.mean(current * current, axis=1, keepdims=True) + 1e-06)
    active = start_index + jnp.arange(orbital_count, dtype=jnp.int32) < kept_count
    return jnp.where(active[:, None], current / magnitude, 0.0).astype(jnp.bfloat16)


def face_selector(planes, width):
    grid = np.arange(planes * PLANE, dtype=np.int32).reshape(planes, P_SIZE, P_SIZE)
    last = P_SIZE - 1
    groups = [
        grid[:, :, 0], grid[:, :, 1], grid[:, 0, :], grid[:, 1, :],
        grid[:, :, last - 1], grid[:, :, last], grid[:, last - 1, :], grid[:, last, :],
    ]
    chosen = jnp.asarray(np.concatenate([g.reshape(-1) for g in groups]))
    points = jnp.arange(width, dtype=jnp.int32)
    return (chosen[:, None] == points[None, :]).astype(jnp.bfloat16)


def transposed_dot(a, b, contract_a, contract_b):
    return lax.dot_general(
        a, b, (((contract_a,), (contract_b,)), ((), ())), preferred_element_type=jnp.float32
    )


def owned_basis(orbitals, potential, kept_count, start_index):
    step = orbitals.shape[0] // CHUNKS
    chunks = []
    tied = None
    for chunk in range(CHUNKS):
        source = orbitals[chunk * step : (chunk + 1) * step]
        if tied is not None:
            source, tied = lax.optimization_barrier((source, tied))
            chunks[-1] = tied
        tied = filtered_basis(source, potential, kept_count, start_index + chunk * step)
        chunks.append(tied)
    return chunks


def cut_kernel(length, *refs):
    out = refs[-1]
    count, _, width = out.shape
    piece = (width - length) // 2
    middle = refs[0].shape[1] // 2
    step = refs[0].shape[0]
    for k, source in enumerate(refs[:-1]):
        rows = pl.ds(k * step, step)
        for s in range(count):
            out[s, rows, :length] = source[:, s * length : (s + 1) * length]
            low = middle - PLANE + s * piece
            out[s, rows, length : length + piece] = source[:, low : low + piece]
            out[s, rows, length + piece :] = source[:, low + PLANE : low + PLANE + piece]


def slab_rows(chunks, length):
    count = HALVES * SLABS
    width = length + 2 * (PLANE // count)
    functions = sum(c.shape[0] for c in chunks)
    whole = pl.BlockSpec(memory_space=pltpu.VMEM)
    slabs = pl.pallas_call(
        functools.partial(cut_kernel, length),
        out_shape=jax.ShapeDtypeStruct((count, functions, width), jnp.bfloat16),
        in_specs=[whole] * len(chunks),
        out_specs=whole,
        compiler_params=pltpu.CompilerParams(vmem_limit_bytes=16 << 20),
    )(*chunks)
    rows = lax.all_to_all(slabs, BOTH, 0, 0, tiled=True)
    return rows.reshape(-1, width)


def pair_swap(value, by, odd):
    devices = lax.axis_size("elem")
    low = [i for i in range(devices) if (i // by) % 2 == odd]
    pairs = [(i, (i + by) % devices) for i in low]
    return lax.ppermute(value, "elem", pairs + [(j, i) for i, j in pairs])


def exchange(value, product, by):
    even = (lax.axis_index("elem") // by) % 2 == 0
    from_odd = pair_swap(jnp.where(even, value, product), by, 1)
    from_even = pair_swap(jnp.where(even, product, value), by, 0)
    ahead = jnp.where(even, from_even, from_odd)
    behind = jnp.where(even, from_odd, from_even)
    return ahead, behind


def scaled(blocks, current, given=None):
    h_self, h_z, h_y = blocks
    back_z = transposed_dot(h_z, current, 0, 0).astype(jnp.bfloat16)
    back_y = transposed_dot(h_y, current, 0, 0).astype(jnp.bfloat16)
    if given is None:
        ahead_z, behind_z = exchange(current, back_z, 1)
        ahead_y, behind_y = exchange(current, back_y, EB)
        running = transposed_dot(h_self, current, 1, 0)
    else:
        ahead_z, ahead_y, running = given
        behind_z = from_behind(back_z, "elem", 1)
        behind_y = from_behind(back_y, "elem", EB)
    running = running + transposed_dot(h_z, ahead_z, 1, 0)
    running = running + transposed_dot(h_y, ahead_y, 1, 0)
    running = running + behind_z.astype(jnp.float32) + behind_y.astype(jnp.float32)
    return (running - SHIFT_CENTER * current.astype(jnp.float32)) / HALF_WIDTH


def slices_of(partial):
    count, total, columns = partial.shape
    return partial.reshape(count, SLABS, total // SLABS, columns).swapaxes(0, 1)


def sum_over_slabs(partial):
    pieces = lax.all_to_all(slices_of(partial), "slab", 0, 0, tiled=True)
    return jnp.sum(pieces.astype(jnp.float32), axis=0).astype(jnp.bfloat16)


def sum_over_halves(summed):
    swapped = swap_halves(summed)
    return (summed.astype(jnp.float32) + swapped.astype(jnp.float32)).astype(jnp.bfloat16)


def gather_slices(summed):
    count, rows, columns = summed.shape
    copies = jnp.broadcast_to(summed[None], (SLABS,) + summed.shape)
    blocks = lax.all_to_all(copies, "slab", 0, 0, tiled=True)
    return [blocks[:, i].reshape(SLABS * rows, columns) for i in range(count)]


def device_body(orbitals, potential, basis_count, states):
    half = lax.axis_index("half")
    slab = lax.axis_index("slab")
    band = half * SLABS + slab
    length = G // (HALVES * SLABS)
    planes = length // PLANE
    slab_potential = lax.dynamic_slice_in_dim(potential[0], band * length, length, 0)

    start = states[0]
    ahead_z = from_behind(start, "elem", -1)
    ahead_y = from_behind(start, "elem", -EB)
    ahead = lax.optimization_barrier(jnp.concatenate([ahead_z, ahead_y]))
    ahead_z, ahead_y = ahead[: ahead.shape[0] // 2], ahead[ahead.shape[0] // 2 :]

    chunks = owned_basis(
        orbitals[0], potential[0], basis_count[0], band * orbitals.shape[1]
    )
    rows = slab_rows(chunks, length)

    above = lax.ppermute(
        rows[:, :PLANE], "slab", [(i + 1, i) for i in range(SLABS - 1)]
    )
    padded = jnp.pad(rows[:, :length].astype(jnp.float32), ((0, 0), (PLANE, PLANE)))
    applied = flat_hamiltonian(padded, length, slab_potential, side_masks(length))
    last = rows[:, length - PLANE : length]
    edges = rows[:, length:]
    swapped_edges = jnp.roll(edges, edges.shape[1] // 2, axis=1)
    h_self = transposed_dot(rows[:, :length], applied.astype(jnp.bfloat16), 1, 1)
    h_self = h_self - transposed_dot(edges, swapped_edges, 1, 1)
    h_self = h_self - transposed_dot(last, above, 1, 1) - transposed_dot(above, last, 1, 1)

    faces = transposed_dot(face_selector(planes, length), rows[:, :length], 1, 1)
    faces = faces.astype(jnp.bfloat16)
    width = 2 * planes * P_SIZE
    other_z = from_behind(faces[:width], "elem", -1)
    other_y = from_behind(faces[width : 2 * width], "elem", -EB)
    weight = -0.5 / PLANE
    h_z = transposed_dot(faces[2 * width : 3 * width], other_z, 0, 0) * weight
    h_y = transposed_dot(faces[3 * width :], other_y, 0, 0) * weight

    summed_self = sum_over_slabs((h_self * (1.0 / G)).astype(jnp.bfloat16)[None])
    whole_self = sum_over_halves(summed_self)
    summed_faces = sum_over_slabs(jnp.stack([h_z, h_y]).astype(jnp.bfloat16))
    whole_faces = sum_over_halves(summed_faces)
    (block_self,) = gather_slices(whole_self)
    running = transposed_dot(block_self, start, 1, 0)
    block_z, block_y = gather_slices(whole_faces)
    blocks = (block_self, block_z, block_y)

    first = scaled(blocks, start, (ahead_z, ahead_y, running)).astype(jnp.bfloat16)
    second = (2.0 * scaled(blocks, first) - start.astype(jnp.float32)).astype(jnp.bfloat16)
    third = 2.0 * scaled(blocks, second) - first.astype(jnp.float32)
    magnitude = jnp.sqrt(jnp.mean(third * third, axis=0, keepdims=True) + 1e-06)
    return (third / magnitude).astype(jnp.bfloat16)[None]


def solution(mesh):
    elems, bands = mesh.devices.shape
    inner = Mesh(mesh.devices.reshape(elems, HALVES, bands // HALVES), ("elem", "half", "slab"))
    placed = (P("elem", BOTH, None), P("elem", None), P("elem"), P("elem", None, BOTH))
    return jax.shard_map(
        device_body, mesh=inner, in_specs=placed, out_specs=P("elem", None, BOTH), check_vma=False
    )
```

```python
import functools

import jax
import jax.numpy as jnp
import numpy as np
from jax import lax
from jax.experimental import pallas as pl
from jax.experimental.pallas import tpu as pltpu
from jax.sharding import Mesh, PartitionSpec as P

P_SIZE = 24
PLANE = P_SIZE * P_SIZE
G = 13824
EB = 4
HALVES = 2
SLABS = 4
CHUNKS = 4
MARGIN = 640
TILE = 2 * PLANE
BOTH = ("half", "slab")

LOW_EDGE = 4.0
HIGH_EDGE = 14.0
SHIFT_CENTER = 4.0
HALF_WIDTH = 6.0
MIDDLE = 0.5 * (HIGH_EDGE + LOW_EDGE)
SPREAD = 0.5 * (HIGH_EDGE - LOW_EDGE)


def from_behind(value, axis, by):
    devices = lax.axis_size(axis)
    return lax.ppermute(value, axis, [(i, (i + by) % devices) for i in range(devices)])


def swap_halves(value):
    return lax.ppermute(value, "half", [(0, 1), (1, 0)])


def side_masks(length):
    where = jnp.arange(length, dtype=jnp.int32)
    zpos = where % P_SIZE
    ypos = where // P_SIZE % P_SIZE
    return (
        (zpos < P_SIZE - 1).astype(jnp.float32),
        (zpos > 0).astype(jnp.float32),
        (ypos < P_SIZE - 1).astype(jnp.float32),
        (ypos > 0).astype(jnp.float32),
    )


def flat_hamiltonian(padded, length, potential, masks):
    values = padded[:, PLANE : PLANE + length]
    beside = padded[:, 2 * PLANE : 2 * PLANE + length] + padded[:, 0:length]
    beside = beside + masks[0] * padded[:, PLANE + 1 : PLANE + 1 + length]
    beside = beside + masks[1] * padded[:, PLANE - 1 : PLANE - 1 + length]
    beside = beside + masks[2] * padded[:, PLANE + P_SIZE : PLANE + P_SIZE + length]
    beside = beside + masks[3] * padded[:, PLANE - P_SIZE : PLANE - P_SIZE + length]
    return 6.0 * values - beside + potential * values


def filter_kernel(length, kept_ref, orbital_ref, potential_ref, mask_ref, out_ref, zero_ref, one_ref, two_ref):
    rows, points = orbital_ref.shape
    count, _, width = out_ref.shape
    piece = (width - length) // 2
    for ref in (zero_ref, one_ref):
        ref[:, :MARGIN] = jnp.zeros((rows, MARGIN), jnp.float32)
        ref[:, MARGIN + points :] = jnp.zeros((rows, MARGIN), jnp.float32)
    for low in range(0, points, TILE):
        zero_ref[:, MARGIN + low : MARGIN + low + TILE] = orbital_ref[
            :, low : low + TILE
        ].astype(jnp.float32)

    def shifted(ref, low, by):
        return ref[:, MARGIN + low + by : MARGIN + low + by + TILE]

    def stencil(ref, low):
        beside = shifted(ref, low, PLANE) + shifted(ref, low, -PLANE)
        for k, by in enumerate((1, -1, P_SIZE, -P_SIZE)):
            beside = beside + mask_ref[k : k + 1, :] * shifted(ref, low, by)
        centre = (6.0 - MIDDLE) + potential_ref[:, low : low + TILE]
        return (centre * shifted(ref, low, 0) - beside) * (1.0 / SPREAD)

    for low in range(0, points, TILE):
        one_ref[:, MARGIN + low : MARGIN + low + TILE] = stencil(zero_ref, low)
    squares = jnp.zeros((rows, TILE), jnp.float32)
    for low in range(0, points, TILE):
        value = 2.0 * stencil(one_ref, low) - shifted(zero_ref, low, 0)
        two_ref[:, low : low + TILE] = value
        squares = squares + value * value
    mean = jnp.sum(squares, axis=1, keepdims=True) * (1.0 / points)
    index = kept_ref[1] + pl.program_id(0) * rows
    index = index + lax.broadcasted_iota(jnp.int32, (rows, 1), 0)
    scale = jnp.where(index < kept_ref[0], 1.0 / jnp.sqrt(mean + 1e-06), 0.0)
    middle = points // 2

    def scaled_span(low, size):
        return (two_ref[:, low : low + size] * scale).astype(jnp.bfloat16)

    for s in range(count):
        out_ref[s, :, :length] = scaled_span(s * length, length)
        low = middle - PLANE + s * piece
        out_ref[s, :, length : length + piece] = scaled_span(low, piece)
        out_ref[s, :, length + piece :] = scaled_span(low + PLANE, piece)


def owned_slabs(orbitals, potential, kept_count, start_index, length):
    count = HALVES * SLABS
    width = length + 2 * (PLANE // count)
    functions, points = orbitals.shape
    step = functions // CHUNKS
    where = np.arange(TILE)
    zpos, ypos = where % P_SIZE, where // P_SIZE % P_SIZE
    masks = [zpos < P_SIZE - 1, zpos > 0, ypos < P_SIZE - 1, ypos > 0]
    masks = jnp.asarray(np.stack(masks).astype(np.float32))
    kept = jnp.stack([kept_count, start_index.astype(jnp.int32)])
    return pl.pallas_call(
        functools.partial(filter_kernel, length),
        out_shape=jax.ShapeDtypeStruct((count, functions, width), jnp.bfloat16),
        grid=(CHUNKS,),
        in_specs=[
            pl.BlockSpec(memory_space=pltpu.SMEM),
            pl.BlockSpec((step, points), lambda c: (c, 0)),
            pl.BlockSpec((1, points), lambda c: (0, 0)),
            pl.BlockSpec((4, TILE), lambda c: (0, 0)),
        ],
        out_specs=pl.BlockSpec((count, step, width), lambda c: (0, c, 0)),
        scratch_shapes=[
            pltpu.VMEM((step, points + 2 * MARGIN), jnp.float32),
            pltpu.VMEM((step, points + 2 * MARGIN), jnp.float32),
            pltpu.VMEM((step, points), jnp.float32),
        ],
        compiler_params=pltpu.CompilerParams(vmem_limit_bytes=24 << 20),
    )(kept, orbitals, potential[None], masks)


def face_selector(planes, width):
    grid = np.arange(planes * PLANE, dtype=np.int32).reshape(planes, P_SIZE, P_SIZE)
    last = P_SIZE - 1
    groups = [
        grid[:, :, 0], grid[:, :, 1], grid[:, 0, :], grid[:, 1, :],
        grid[:, :, last - 1], grid[:, :, last], grid[:, last - 1, :], grid[:, last, :],
    ]
    chosen = jnp.asarray(np.concatenate([g.reshape(-1) for g in groups]))
    points = jnp.arange(width, dtype=jnp.int32)
    return (chosen[:, None] == points[None, :]).astype(jnp.bfloat16)


def transposed_dot(a, b, contract_a, contract_b):
    return lax.dot_general(
        a, b, (((contract_a,), (contract_b,)), ((), ())), preferred_element_type=jnp.float32
    )


def slab_rows(slabs):
    rows = lax.all_to_all(slabs, BOTH, 0, 0, tiled=True)
    return rows.reshape(-1, rows.shape[2])


def pair_swap(value, by, odd):
    devices = lax.axis_size("elem")
    low = [i for i in range(devices) if (i // by) % 2 == odd]
    pairs = [(i, (i + by) % devices) for i in low]
    return lax.ppermute(value, "elem", pairs + [(j, i) for i, j in pairs])


def exchange(value, product, by):
    even = (lax.axis_index("elem") // by) % 2 == 0
    from_odd = pair_swap(jnp.where(even, value, product), by, 1)
    from_even = pair_swap(jnp.where(even, product, value), by, 0)
    ahead = jnp.where(even, from_even, from_odd)
    behind = jnp.where(even, from_odd, from_even)
    return ahead, behind


def scaled(blocks, current, given=None):
    h_self, h_z, h_y = blocks
    back_z = transposed_dot(h_z, current, 0, 0).astype(jnp.bfloat16)
    back_y = transposed_dot(h_y, current, 0, 0).astype(jnp.bfloat16)
    if given is None:
        ahead_z, behind_z = exchange(current, back_z, 1)
        ahead_y, behind_y = exchange(current, back_y, EB)
        running = transposed_dot(h_self, current, 1, 0)
    else:
        ahead_z, ahead_y, running = given
        behind_z = from_behind(back_z, "elem", 1)
        behind_y = from_behind(back_y, "elem", EB)
    running = running + transposed_dot(h_z, ahead_z, 1, 0)
    running = running + transposed_dot(h_y, ahead_y, 1, 0)
    running = running + behind_z.astype(jnp.float32) + behind_y.astype(jnp.float32)
    return (running - SHIFT_CENTER * current.astype(jnp.float32)) / HALF_WIDTH


def slices_of(partial):
    count, total, columns = partial.shape
    return partial.reshape(count, SLABS, total // SLABS, columns).swapaxes(0, 1)


def sum_over_slabs(partial):
    pieces = lax.all_to_all(slices_of(partial), "slab", 0, 0, tiled=True)
    return jnp.sum(pieces.astype(jnp.float32), axis=0).astype(jnp.bfloat16)


def sum_over_halves(summed):
    swapped = swap_halves(summed)
    return (summed.astype(jnp.float32) + swapped.astype(jnp.float32)).astype(jnp.bfloat16)


def gather_slices(summed):
    count, rows, columns = summed.shape
    copies = jnp.broadcast_to(summed[None], (SLABS,) + summed.shape)
    blocks = lax.all_to_all(copies, "slab", 0, 0, tiled=True)
    return [blocks[:, i].reshape(SLABS * rows, columns) for i in range(count)]


def device_body(orbitals, potential, basis_count, states):
    half = lax.axis_index("half")
    slab = lax.axis_index("slab")
    band = half * SLABS + slab
    length = G // (HALVES * SLABS)
    planes = length // PLANE
    slab_potential = lax.dynamic_slice_in_dim(potential[0], band * length, length, 0)

    start = states[0]
    ahead_z = from_behind(start, "elem", -1)
    ahead_y = from_behind(start, "elem", -EB)
    ahead = lax.optimization_barrier(jnp.concatenate([ahead_z, ahead_y]))
    ahead_z, ahead_y = ahead[: ahead.shape[0] // 2], ahead[ahead.shape[0] // 2 :]

    slabs = owned_slabs(
        orbitals[0], potential[0], basis_count[0], band * orbitals.shape[1], length
    )
    rows = slab_rows(slabs)

    above = lax.ppermute(
        rows[:, :PLANE], "slab", [(i + 1, i) for i in range(SLABS - 1)]
    )
    masks = side_masks(length)
    padded = jnp.pad(rows[:, :length].astype(jnp.float32), ((0, 0), (PLANE, PLANE)))
    applied = flat_hamiltonian(padded, length, slab_potential, masks)
    applied = applied.astype(jnp.bfloat16)
    applied, rows = lax.optimization_barrier((applied, rows))

    faces = transposed_dot(face_selector(planes, length), rows[:, :length], 1, 1)
    faces = faces.astype(jnp.bfloat16)
    width = 2 * planes * P_SIZE
    other_z = from_behind(faces[:width], "elem", -1)
    other_y = from_behind(faces[width : 2 * width], "elem", -EB)
    last = rows[:, length - PLANE : length]
    edges = rows[:, length:]
    swapped_edges = jnp.roll(edges, edges.shape[1] // 2, axis=1)
    h_self = transposed_dot(rows[:, :length], applied, 1, 1)
    h_self = h_self - transposed_dot(edges, swapped_edges, 1, 1)
    h_self = h_self - transposed_dot(last, above, 1, 1) - transposed_dot(above, last, 1, 1)
    weight = -0.5 / PLANE
    h_z = transposed_dot(faces[2 * width : 3 * width], other_z, 0, 0) * weight
    h_y = transposed_dot(faces[3 * width :], other_y, 0, 0) * weight

    summed_self = sum_over_slabs((h_self * (1.0 / G)).astype(jnp.bfloat16)[None])
    whole_self = sum_over_halves(summed_self)
    summed_faces = sum_over_slabs(jnp.stack([h_z, h_y]).astype(jnp.bfloat16))
    whole_faces = sum_over_halves(summed_faces)
    (block_self,) = gather_slices(whole_self)
    running = transposed_dot(block_self, start, 1, 0)
    block_z, block_y = gather_slices(whole_faces)
    blocks = (block_self, block_z, block_y)

    first = scaled(blocks, start, (ahead_z, ahead_y, running)).astype(jnp.bfloat16)
    second = (2.0 * scaled(blocks, first) - start.astype(jnp.float32)).astype(jnp.bfloat16)
    third = 2.0 * scaled(blocks, second) - first.astype(jnp.float32)
    magnitude = jnp.sqrt(jnp.mean(third * third, axis=0, keepdims=True) + 1e-06)
    return (third / magnitude).astype(jnp.bfloat16)[None]


def solution(mesh):
    elems, bands = mesh.devices.shape
    inner = Mesh(mesh.devices.reshape(elems, HALVES, bands // HALVES), ("elem", "half", "slab"))
    placed = (P("elem", BOTH, None), P("elem", None), P("elem"), P("elem", None, BOTH))
    return jax.shard_map(
        device_body, mesh=inner, in_specs=placed, out_specs=P("elem", None, BOTH), check_vma=False
    )
```

```python
import functools

import jax
import jax.numpy as jnp
import numpy as np
from jax import lax
from jax.experimental import pallas as pl
from jax.experimental.pallas import tpu as pltpu
from jax.sharding import Mesh, PartitionSpec as P

P_SIZE = 24
PLANE = P_SIZE * P_SIZE
G = 13824
EB = 4
HALVES = 2
SLABS = 4
CHUNKS = 4
BOTH = ("half", "slab")

LOW_EDGE = 4.0
HIGH_EDGE = 14.0
SHIFT_CENTER = 4.0
HALF_WIDTH = 6.0
MIDDLE = 0.5 * (HIGH_EDGE + LOW_EDGE)
SPREAD = 0.5 * (HIGH_EDGE - LOW_EDGE)


def from_behind(value, axis, by):
    devices = lax.axis_size(axis)
    return lax.ppermute(value, axis, [(i, (i + by) % devices) for i in range(devices)])


def swap_halves(value):
    return lax.ppermute(value, "half", [(0, 1), (1, 0)])


def side_masks(length):
    where = jnp.arange(length, dtype=jnp.int32)
    zpos = where % P_SIZE
    ypos = where // P_SIZE % P_SIZE
    return (
        (zpos < P_SIZE - 1).astype(jnp.float32),
        (zpos > 0).astype(jnp.float32),
        (ypos < P_SIZE - 1).astype(jnp.float32),
        (ypos > 0).astype(jnp.float32),
    )


def flat_hamiltonian(padded, length, potential, masks):
    values = padded[:, PLANE : PLANE + length]
    beside = padded[:, 2 * PLANE : 2 * PLANE + length] + padded[:, 0:length]
    beside = beside + masks[0] * padded[:, PLANE + 1 : PLANE + 1 + length]
    beside = beside + masks[1] * padded[:, PLANE - 1 : PLANE - 1 + length]
    beside = beside + masks[2] * padded[:, PLANE + P_SIZE : PLANE + P_SIZE + length]
    beside = beside + masks[3] * padded[:, PLANE - P_SIZE : PLANE - P_SIZE + length]
    return 6.0 * values - beside + potential * values


def whole_hamiltonian(values, potential, masks):
    padded = jnp.pad(values, ((0, 0), (PLANE, PLANE)))
    return flat_hamiltonian(padded, values.shape[1], potential, masks)


def filtered_basis(orbitals, potential, kept_count, start_index):
    orbital_count = orbitals.shape[0]
    masks = side_masks(G)
    previous = orbitals.astype(jnp.float32)
    current = (whole_hamiltonian(previous, potential, masks) - MIDDLE * previous) / SPREAD
    current = (
        2.0 * (whole_hamiltonian(current, potential, masks) - MIDDLE * current) / SPREAD - previous
    )
    magnitude = jnp.sqrt(jnp.mean(current * current, axis=1, keepdims=True) + 1e-06)
    active = start_index + jnp.arange(orbital_count, dtype=jnp.int32) < kept_count
    return jnp.where(active[:, None], current / magnitude, 0.0).astype(jnp.bfloat16)


def face_selector(planes, width):
    grid = np.arange(planes * PLANE, dtype=np.int32).reshape(planes, P_SIZE, P_SIZE)
    last = P_SIZE - 1
    groups = [
        grid[:, :, 0], grid[:, :, 1], grid[:, 0, :], grid[:, 1, :],
        grid[:, :, last - 1], grid[:, :, last], grid[:, last - 1, :], grid[:, last, :],
    ]
    chosen = jnp.asarray(np.concatenate([g.reshape(-1) for g in groups]))
    points = jnp.arange(width, dtype=jnp.int32)
    return (chosen[:, None] == points[None, :]).astype(jnp.bfloat16)


def transposed_dot(a, b, contract_a, contract_b):
    return lax.dot_general(
        a, b, (((contract_a,), (contract_b,)), ((), ())), preferred_element_type=jnp.float32
    )


def owned_basis(orbitals, potential, kept_count, start_index):
    step = orbitals.shape[0] // CHUNKS
    chunks = []
    tied = None
    for chunk in range(CHUNKS):
        if tied is not None:
            orbitals, tied = lax.optimization_barrier((orbitals, tied))
            chunks[-1] = tied
        source = orbitals[chunk * step : (chunk + 1) * step]
        tied = filtered_basis(source, potential, kept_count, start_index + chunk * step)
        chunks.append(tied)
    return chunks


def cut_kernel(length, *refs):
    out = refs[-1]
    count, _, width = out.shape
    piece = (width - length) // 2
    middle = refs[0].shape[1] // 2
    step = refs[0].shape[0]
    for k, source in enumerate(refs[:-1]):
        rows = pl.ds(k * step, step)
        for s in range(count):
            out[s, rows, :length] = source[:, s * length : (s + 1) * length]
            low = middle - PLANE + s * piece
            out[s, rows, length : length + piece] = source[:, low : low + piece]
            out[s, rows, length + piece :] = source[:, low + PLANE : low + PLANE + piece]


def slab_rows(chunks, length):
    count = HALVES * SLABS
    width = length + 2 * (PLANE // count)
    functions = sum(c.shape[0] for c in chunks)
    whole = pl.BlockSpec(memory_space=pltpu.VMEM)
    slabs = pl.pallas_call(
        functools.partial(cut_kernel, length),
        out_shape=jax.ShapeDtypeStruct((count, functions, width), jnp.bfloat16),
        in_specs=[whole] * len(chunks),
        out_specs=whole,
        compiler_params=pltpu.CompilerParams(vmem_limit_bytes=16 << 20),
    )(*chunks)
    rows = lax.all_to_all(slabs, BOTH, 0, 0, tiled=True)
    return rows.reshape(-1, width)


def pair_swap(value, by, odd):
    devices = lax.axis_size("elem")
    low = [i for i in range(devices) if (i // by) % 2 == odd]
    pairs = [(i, (i + by) % devices) for i in low]
    return lax.ppermute(value, "elem", pairs + [(j, i) for i, j in pairs])


def exchange(value, product, by):
    even = (lax.axis_index("elem") // by) % 2 == 0
    from_odd = pair_swap(jnp.where(even, value, product), by, 1)
    from_even = pair_swap(jnp.where(even, product, value), by, 0)
    ahead = jnp.where(even, from_even, from_odd)
    behind = jnp.where(even, from_odd, from_even)
    return ahead, behind


def scaled(blocks, current, given=None):
    h_self, h_z, h_y = blocks
    back_z = transposed_dot(h_z, current, 0, 0).astype(jnp.bfloat16)
    back_y = transposed_dot(h_y, current, 0, 0).astype(jnp.bfloat16)
    if given is None:
        ahead_z, behind_z = exchange(current, back_z, 1)
        ahead_y, behind_y = exchange(current, back_y, EB)
        running = transposed_dot(h_self, current, 1, 0)
    else:
        ahead_z, ahead_y, running = given
        behind_y = from_behind(back_y, "elem", EB)
        behind_z = from_behind(back_z, "elem", 1)
    running = running + transposed_dot(h_z, ahead_z, 1, 0)
    running = running + transposed_dot(h_y, ahead_y, 1, 0)
    running = running + behind_z.astype(jnp.float32) + behind_y.astype(jnp.float32)
    return (running - SHIFT_CENTER * current.astype(jnp.float32)) / HALF_WIDTH


def slices_of(partial):
    count, total, columns = partial.shape
    return partial.reshape(count, SLABS, total // SLABS, columns).swapaxes(0, 1)


def sum_over_slabs(partial):
    pieces = lax.all_to_all(slices_of(partial), "slab", 0, 0, tiled=True)
    return jnp.sum(pieces.astype(jnp.float32), axis=0).astype(jnp.bfloat16)


def sum_over_halves(summed):
    swapped = swap_halves(summed)
    return (summed.astype(jnp.float32) + swapped.astype(jnp.float32)).astype(jnp.bfloat16)


def gather_slices(summed):
    count, rows, columns = summed.shape
    copies = jnp.broadcast_to(summed[None], (SLABS,) + summed.shape)
    blocks = lax.all_to_all(copies, "slab", 0, 0, tiled=True)
    return [blocks[:, i].reshape(SLABS * rows, columns) for i in range(count)]


def device_body(orbitals, potential, basis_count, states):
    half = lax.axis_index("half")
    slab = lax.axis_index("slab")
    band = half * SLABS + slab
    length = G // (HALVES * SLABS)
    planes = length // PLANE
    slab_potential = lax.dynamic_slice_in_dim(potential[0], band * length, length, 0)

    start = states[0]
    ahead_z = from_behind(start, "elem", -1)
    ahead_y = from_behind(start, "elem", -EB)
    ahead = lax.optimization_barrier(jnp.concatenate([ahead_z, ahead_y]))
    ahead_z, ahead_y = ahead[: ahead.shape[0] // 2], ahead[ahead.shape[0] // 2 :]

    chunks = owned_basis(
        orbitals[0], potential[0], basis_count[0], band * orbitals.shape[1]
    )
    rows = slab_rows(chunks, length)

    above = lax.ppermute(
        rows[:, :PLANE], "slab", [(i + 1, i) for i in range(SLABS - 1)]
    )
    masks = side_masks(length)
    padded = jnp.pad(rows[:, :length].astype(jnp.float32), ((0, 0), (PLANE, PLANE)))
    applied = flat_hamiltonian(padded, length, slab_potential, masks)
    applied = applied.astype(jnp.bfloat16)
    applied = lax.optimization_barrier(applied)

    faces = transposed_dot(face_selector(planes, length), rows[:, :length], 1, 1)
    faces = faces.astype(jnp.bfloat16)
    width = 2 * planes * P_SIZE
    other_z = from_behind(faces[:width], "elem", -1)
    other_y = from_behind(faces[width : 2 * width], "elem", -EB)
    last = rows[:, length - PLANE : length]
    edges = rows[:, length:]
    swapped_edges = jnp.roll(edges, edges.shape[1] // 2, axis=1)
    h_self = transposed_dot(rows[:, :length], applied, 1, 1)
    h_self = h_self - transposed_dot(edges, swapped_edges, 1, 1)
    h_self = h_self - transposed_dot(last, above, 1, 1) - transposed_dot(above, last, 1, 1)
    weight = -0.5 / PLANE
    h_z = transposed_dot(faces[2 * width : 3 * width], other_z, 0, 0) * weight
    h_y = transposed_dot(faces[3 * width :], other_y, 0, 0) * weight

    summed_self = sum_over_slabs((h_self * (1.0 / G)).astype(jnp.bfloat16)[None])
    whole_self = sum_over_halves(summed_self)
    summed_faces = sum_over_slabs(jnp.stack([h_z, h_y]).astype(jnp.bfloat16))
    whole_faces = sum_over_halves(summed_faces)
    (block_self,) = gather_slices(whole_self)
    running = transposed_dot(block_self, start, 1, 0)
    block_z, block_y = gather_slices(whole_faces)
    blocks = (block_self, block_z, block_y)

    first = scaled(blocks, start, (ahead_z, ahead_y, running)).astype(jnp.bfloat16)
    second = (2.0 * scaled(blocks, first) - start.astype(jnp.float32)).astype(jnp.bfloat16)
    third = 2.0 * scaled(blocks, second) - first.astype(jnp.float32)
    magnitude = jnp.sqrt(jnp.mean(third * third, axis=0, keepdims=True) + 1e-06)
    return (third / magnitude).astype(jnp.bfloat16)[None]


def solution(mesh):
    elems, bands = mesh.devices.shape
    inner = Mesh(mesh.devices.reshape(elems, HALVES, bands // HALVES), ("elem", "half", "slab"))
    placed = (P("elem", BOTH, None), P("elem", None), P("elem"), P("elem", None, BOTH))
    return jax.shard_map(
        device_body, mesh=inner, in_specs=placed, out_specs=P("elem", None, BOTH), check_vma=False
    )
```
